32 devices in a mesh: sector: 8 (over y, x, core), term: 4 (over z).
Axes of the slice: x: 2, y: 2, z: 4, core: 2. Of those that a mesh axis runs over, the one named last changes fastest.
Arguments:
- wave: float32 [8, 512, 512], P('sector', 'term'), may hold values from -12 to 12
- left_ops: bfloat16 [16, 8, 512, 512], P('term', 'sector'), may hold values from -4 to 4
- right_ops: bfloat16 [16, 8, 512, 512], P('term', 'sector'), may hold values from -4 to 4
- charges: int32 [16], replicated, may hold values from -1 to 1, as said below
- diag: float32 [8, 512, 512], P('sector', 'term'), may hold values from 0.5 to 8
Outputs:
- psi_out: float32 [8, 512, 512], P('sector', 'term')
The draws below stay inside these ranges and needn't reach their ends.
Inputs may be any that keep to these rules, and one draw needn't show every extreme that they name: `charges`: exactly (17) // 2 terms have charge 0; at least one term has charge 1 and at least one has charge -1.
All inputs are finite; a program needn't handle non-finite values.
Results may differ from the reference program's by a relative error of at most 0.0085.
Values may be sent and summed in bfloat16 or wider, within the bound.
No kernel may reach another device: no remote copies, remote signals or barrier semaphores. Data moves between devices by JAX's collectives and lax.ppermute only.
A program may use at most 64 MiB of HBM per device.

```python
import jax
import jax.numpy as jnp
from jax import lax

SECT = 512
STEPS = 3
SECTORS = 8
TERMS = 16


def sector_gains(key):
    gain_key = jax.random.fold_in(key, 7)
    uniform_draw = jax.random.uniform(gain_key, (SECTORS,), jnp.float32)
    lowest, highest = (0.75, 6.0)
    strength = jnp.exp(jnp.log(lowest) + uniform_draw * (jnp.log(highest) - jnp.log(lowest)))
    return jnp.sqrt(2.0 * strength / TERMS)


def environment(key, salt):
    sector_gain = sector_gains(key)
    noise_key = jax.random.fold_in(key, salt)
    noise_part = jnp.clip(jax.random.normal(noise_key, (TERMS, SECTORS, SECT, SECT), jnp.float32), -6.0, 6.0)
    noise_part = noise_part / jnp.sqrt(jnp.float32(SECT))
    identity = jnp.eye(SECT, dtype=jnp.float32)
    blocks = noise_part + sector_gain[None, :, None, None] * identity[None, None]
    return blocks.astype(jnp.bfloat16)


def draw_left_ops(key, part):
    return environment(key, 11)


def draw_right_ops(key, part):
    return environment(key, 13)


def draw_wave(key, part):
    scale_key = jax.random.fold_in(key, 23)
    entry_key = jax.random.fold_in(key, 29)
    uniform_draw = jax.random.uniform(scale_key, (SECTORS,), jnp.float32)
    amplitude = jnp.exp(jnp.log(0.5) + uniform_draw * (jnp.log(2.0) - jnp.log(0.5)))
    entries = jnp.clip(jax.random.normal(entry_key, (SECTORS, SECT, SECT), jnp.float32), -6.0, 6.0)
    return (entries * amplitude[:, None, None]).astype(jnp.float32)


def draw_charges(key, part):
    ordering = jax.random.permutation(jax.random.fold_in(key, 17), TERMS)
    sign_draw = 2 * jax.random.randint(jax.random.fold_in(key, 19), (TERMS,), 0, 2) - 1
    zero_count = (TERMS + 1) // 2
    position = jnp.arange(TERMS, dtype=jnp.int32)
    by_position = jnp.where(position < zero_count, 0, jnp.where(position == zero_count, 1, jnp.where(position == zero_count + 1, -1, sign_draw)))
    charge_list = jnp.zeros((TERMS,), jnp.int32).at[ordering].set(by_position.astype(jnp.int32))
    return charge_list.astype(jnp.int32)


def block_scale(key, shape, pieces, least, top_value):
    factor_of, own = 1.0, jax.random.fold_in(key, 6)
    for dim, shards_of in pieces:
        heights = jnp.exp(jax.random.uniform(jax.random.fold_in(own, dim), (shards_of,), jnp.float32, least / len(pieces), top_value / len(pieces)))
        factor_of = factor_of * jnp.repeat(heights, shape[dim] // shards_of).reshape([-1 if axis == dim else 1 for axis in range(len(shape))])
    return factor_of


def setup_inputs(seed: int = 0) -> dict:
    key_of = jax.random.split(jax.random.key(seed), 6)
    return {
        "wave": draw_wave(jax.random.fold_in(key_of[5], 71), 0),
        "left_ops": draw_left_ops(jax.random.fold_in(key_of[5], 71), 0),
        "right_ops": draw_right_ops(jax.random.fold_in(key_of[5], 71), 0),
        "charges": draw_charges(jax.random.fold_in(key_of[5], 71), 0),
        "diag": jnp.clip(0.5 + 7.5 * jax.random.uniform(key_of[4], (SECTORS, SECT, SECT), jnp.float32) ** block_scale(key_of[4], (SECTORS, SECT, SECT), ((0, 8), (1, 4)), -0.2, 0.2), 0.5, 8.0),
    }


def reference(wave, left_ops, right_ops, charges, diag):
    psi = wave
    zero_block = jnp.zeros((1, SECT, SECT), jnp.bfloat16)
    for step in range(STEPS):
        wb = psi.astype(jnp.bfloat16)
        lower = jnp.concatenate([zero_block, wb[:-1]], axis=0)
        upper = jnp.concatenate([wb[1:], zero_block], axis=0)

        def add_term(acc, items):
            left, right, charge = items
            source = jnp.where(charge == 1, lower, jnp.where(charge == -1, upper, wb))
            inner = jnp.einsum('sij,sjk->sik', left.astype(jnp.float32), source.astype(jnp.float32)).astype(jnp.bfloat16)
            image = jnp.einsum('sij,skj->sik', inner.astype(jnp.float32), right.astype(jnp.float32))
            return (acc + image, None)
        hpsi, unused = lax.scan(add_term, jnp.zeros(psi.shape, jnp.float32), (left_ops, right_ops, charges))
        theta = jnp.sum(psi * hpsi) / jnp.sum(psi * psi)
        fresh = psi - (hpsi - theta * psi) / jnp.maximum(jnp.abs(diag - theta), 1.0)
        psi = fresh / jnp.sqrt(jnp.mean(fresh * fresh) + 1e-06)
    return psi
```

```python
import functools

import jax
import jax.numpy as jnp
from jax import lax
from jax.experimental import pallas as pl
from jax.experimental.pallas import tpu as pltpu
from jax.sharding import PartitionSpec as P

STEPS = 3
F32, BF16 = jnp.float32, jnp.bfloat16
NT = (((1,), (1,)), ((), ()))
VMEM = pl.BlockSpec(memory_space=pltpu.VMEM)
SMEM = pl.BlockSpec(memory_space=pltpu.SMEM)
PARAMS = pltpu.CompilerParams(vmem_limit_bytes=40 << 20)


def exchange(value, k):
    count = lax.axis_size("term")
    return lax.ppermute(value, "term", [(i, i ^ k) for i in range(count)])


def swap_near(value):
    count = lax.axis_size("sector")
    return lax.ppermute(value, "sector", [(i, i ^ 1) for i in range(count)])


def swap_far(value):
    count = lax.axis_size("sector")
    return lax.ppermute(
        value, "sector", [(i, (i + 1 if i % 2 else i - 1) % count) for i in range(count)]
    )


def lane_sums(*values):
    lane = lax.broadcasted_iota(jnp.int32, (1, 128), 1)
    row = jnp.zeros((1, 128), F32)
    for i, value in enumerate(values):
        row = jnp.where(lane == i, value, row)
    return row


def total(v):
    return jnp.sum(jnp.sum(v, axis=1, keepdims=True), axis=0, keepdims=True)


def matmul_kernel(groups, sel, left, right, *refs):
    n_own = groups
    own = refs[:n_own]
    near, far_a, far_b, stats = refs[n_own : n_own + 4]
    mine = refs[n_own + 4]
    away = refs[n_own + 5 : 2 * n_own + 4]
    row = refs[2 * n_own + 4]
    src, acc = refs[2 * n_own + 5 :]
    terms, size = left.shape[0], left.shape[1]
    rows = size // groups
    place = sel[terms + 2]
    half = far_a.shape[0]
    for k in range(groups):
        at = pl.ds(pl.multiple_of((place ^ k) * rows, rows), rows)
        src[1, at] = own[k][...]
        src[sel[terms], at] = near[k]
        src[sel[terms + 1], at] = far_a[k] if k < half else far_b[k - half]
    src[3] = jnp.zeros((size, size), BF16)
    for t in range(terms):
        inner = jnp.dot(left[t], src[sel[t]], preferred_element_type=F32).astype(BF16)
        image = lax.dot_general(inner, right[t], NT, preferred_element_type=F32)
        if t == 0:
            acc[...] = image
        else:
            acc[...] += image
    cross = total(acc[...] * src[1].astype(F32))
    row[...] = stats[...] + lane_sums(cross)
    for k in range(groups):
        at = pl.ds(pl.multiple_of((place ^ k) * rows, rows), rows)
        if k == 0:
            mine[...] = acc[at]
        else:
            away[k - 1][...] = acc[at].astype(BF16)


def apply_terms(sel, left, right, own, near, far_a, far_b, stats):
    groups = len(own)
    rows, size = own[0].shape
    return pl.pallas_call(
        functools.partial(matmul_kernel, groups),
        out_shape=[jax.ShapeDtypeStruct((rows, size), F32)]
        + [jax.ShapeDtypeStruct((rows, size), BF16)] * (groups - 1)
        + [jax.ShapeDtypeStruct((1, 128), F32)],
        in_specs=[SMEM] + [VMEM] * (groups + 6),
        out_specs=[VMEM] * (groups + 1),
        scratch_shapes=[pltpu.VMEM((4, size, size), BF16), pltpu.VMEM((size, size), F32)],
        compiler_params=PARAMS,
        name="apply_terms",
    )(sel, left, right, *own, near, far_a, far_b, stats)


def update_kernel(count, n_away, first, sums, fresh, diag, mine, *refs):
    away = refs[:n_away]
    new, rounded, stats = refs[n_away:]
    image = mine[...]
    for ref in away:
        image = image + ref[...].astype(F32)
    table = jnp.sum(sums[...], axis=0)
    theta = table[:, 0:1] / table[:, 1:2]
    old = fresh[...]
    value = old - (image - theta * old) / jnp.maximum(jnp.abs(diag[...] - theta), 1.0)
    if not first:
        value = value / jnp.sqrt(table[:, 2:3] / count + 1e-06)
    new[...] = value
    low = value.astype(BF16)
    rounded[...] = low
    stats[...] = lane_sums(0.0, total(low.astype(F32) * value), total(value * value))


def update(count, first, sums, fresh, diag, mine, away):
    shape = fresh.shape
    return pl.pallas_call(
        functools.partial(update_kernel, count, len(away), first),
        out_shape=[
            jax.ShapeDtypeStruct(shape, F32),
            jax.ShapeDtypeStruct(shape, BF16),
            jax.ShapeDtypeStruct((1, 128), F32),
        ],
        in_specs=[VMEM] * (4 + len(away)),
        out_specs=[VMEM] * 3,
        compiler_params=PARAMS,
        name="update",
    )(sums, fresh, diag, mine, *away)


def everyone(row):
    axes = ("sector", "term")
    count = lax.axis_size(axes)
    return lax.all_to_all(jnp.broadcast_to(row[None], (count, 1, 128)), axes, 0, 0)


def per_device(wave, left_ops, right_ops, charges, diag):
    terms = left_ops.shape[0]
    left, right = left_ops[:, 0], right_ops[:, 0]
    groups, sectors = lax.axis_size("term"), lax.axis_size("sector")
    place, sector = lax.axis_index("term"), lax.axis_index("sector")
    moved = lax.dynamic_slice_in_dim(charges, place * terms, terms)
    inside = (sector - moved >= 0) & (sector - moved < sectors)
    source = jnp.where(inside, moved + 1, 3)
    odd = sector % 2
    sel = jnp.concatenate([source, jnp.stack([2 * odd, 2 - 2 * odd, place])]).astype(jnp.int32)

    fresh, rows = wave[0], diag[0]
    count = fresh.size * groups * sectors
    rounded = fresh.astype(BF16)
    stats = lane_sums(0.0, jnp.sum(rounded.astype(F32) * fresh), jnp.sum(fresh * fresh))
    for step in range(STEPS):
        own = [rounded] + [exchange(rounded, k) for k in range(1, groups)]
        half = groups // 2
        far_a = swap_far(jnp.stack(own[:half]))
        far_b = swap_far(jnp.stack(own[half:]))
        near = swap_near(jnp.stack(own))
        mine, *rest = apply_terms(sel, left, right, own, near, far_a, far_b, stats)
        away, row = rest[:-1], rest[-1]
        got = [exchange(away[k - 1], k) for k in range(groups - 1, 0, -1)]
        sums = everyone(row)
        fresh, rounded, stats = update(count, step == 0, sums, fresh, rows, mine, got)
    sums = everyone(stats)
    norm = jnp.sum(sums, axis=0)[0, 2]
    return (fresh / jnp.sqrt(norm / count + 1e-06))[None]


def solution(mesh):
    in_specs = (
        P("sector", "term", None),
        P("term", "sector", None, None),
        P("term", "sector", None, None),
        P(),
        P("sector", "term", None),
    )
    out_specs = P("sector", "term", None)
    return jax.shard_map(
        per_device, mesh=mesh, in_specs=in_specs, out_specs=out_specs, check_vma=False
    )
```
